32 devices in a mesh: tm: 8 (over z, y), mp: 4 (over x, core).
Axes of the slice: x: 2, y: 2, z: 4, core: 2. Of those that a mesh axis runs over, the one named last changes fastest.
Arguments:
- queries: bfloat16 [1536, 1024], P('tm', 'mp'), may hold values from -8 to 8
- d_queries: bfloat16 [1536, 1024], P('tm', 'mp'), may hold values from -6 to 6
- key_rows: bfloat16 [1536, 1024], P('tm', 'mp'), may hold values from -8 to 8
- value_rows: bfloat16 [1536, 1024], P('tm', 'mp'), may hold values from -6 to 6
- d_key_rows: bfloat16 [1536, 1024], P('tm', 'mp'), may hold values from -6 to 6
- d_value_rows: bfloat16 [1536, 1024], P('tm', 'mp'), may hold values from -6 to 6
- live_flags: int32 [1536], P('tm'), may hold values from 0 to 1, as said below
- out_weight: bfloat16 [1024, 5120], P('mp'), may hold values from -1 to 1
- gate_scale: float32 [5120], P('mp'), may hold values from 0.25 to 1.75
- tokens: bfloat16 [1536, 5120], P('tm', 'mp'), may hold values from -6 to 6
- d_tokens: bfloat16 [1536, 5120], P('tm', 'mp'), may hold values from -6 to 6
Outputs:
- result: bfloat16 [1536, 5120], P('tm', 'mp')
- d_result: bfloat16 [1536, 5120], P('tm', 'mp')
The draws below stay inside these ranges and needn't reach their ends.
Inputs may be any that keep to these rules, and one draw needn't show every extreme that they name: live_flags are equal within each aligned run of 32 tokens.
All inputs are finite; a program needn't handle non-finite values.
Results may differ from the reference program's by a relative error of at most 0.019.
Values may be sent and summed in bfloat16 or wider, within the bound.
A program may use at most 128 MiB of HBM per device.

```python
import math
import jax
import jax.numpy as jnp
from jax import lax

D = 5120
HD = 128
H_DEV = 2
FRAME = 32
HEADS = 8
TOKENS = 1536
N_MP = 4


def drawn_field(key):
    values = 1.2 * jax.random.normal(key, (TOKENS, HEADS * HD), jnp.float32)
    return values


def draw_queries(key, part):
    values = drawn_field(jax.random.fold_in(key, 11))
    return jnp.clip(values, -8.0, 8.0).astype(jnp.bfloat16)


def draw_key_rows(key, part):
    values = drawn_field(jax.random.fold_in(key, 13))
    return jnp.clip(values, -8.0, 8.0).astype(jnp.bfloat16)


def draw_live_flags(key, part):
    frames = jax.random.randint(jax.random.fold_in(key, 17), (TOKENS // FRAME,), 0, 4)
    flags = (frames > 0).astype(jnp.int32)
    return jnp.repeat(flags, FRAME)


def levels(rng, dims, cuts, least, top_value):
    def one(axis_at, shards_of):
        draws = jax.random.uniform(jax.random.fold_in(jax.random.fold_in(rng, 6), axis_at), (shards_of,), jnp.float32, least / len(cuts), top_value / len(cuts))
        return jnp.repeat(jnp.exp(draws), dims[axis_at] // shards_of).reshape((-1,) + (1,) * (len(dims) - axis_at - 1))

    loudness = one(*cuts[0])
    for cut in cuts[1:]:
        loudness = loudness * one(*cut)
    return loudness


def noise(own_key, extent, spread, most, cuts=(), dtype=jnp.bfloat16):
    drawn = jax.random.normal(own_key, extent, jnp.float32) * spread
    if len(cuts) > 0:
        drawn = levels(own_key, extent, cuts, -0.22, 0.18) * drawn
    return jnp.clip(drawn, min=-most, max=most).astype(dtype)


def setup_inputs(seed: int = 0) -> dict:
    seeds = jax.random.split(jax.random.key(seed), 12)
    return {
        "queries": draw_queries(jax.random.fold_in(seeds[11], 71), 0),
        "d_queries": noise(seeds[1], (TOKENS, HEADS * HD), 1.0, 6.0, ((0, 8), (1, 4))),
        "key_rows": draw_key_rows(jax.random.fold_in(seeds[11], 71), 0),
        "value_rows": noise(seeds[3], (TOKENS, HEADS * HD), 1.0, 6.0, ((0, 8), (1, 4))),
        "d_key_rows": noise(seeds[4], (TOKENS, HEADS * HD), 1.0, 6.0, ((0, 8), (1, 4))),
        "d_value_rows": noise(seeds[5], (TOKENS, HEADS * HD), 1.0, 6.0, ((0, 8), (1, 4))),
        "live_flags": draw_live_flags(jax.random.fold_in(seeds[11], 71), 0),
        "out_weight": noise(seeds[7], (HEADS * HD, D), (H_DEV * HD // 8) ** -0.5, 1.0, ((0, 4),)),
        "gate_scale": jnp.clip(1.0 + 0.15 * jax.random.normal(seeds[8], (D,), jnp.float32), 0.25, 1.75),
        "tokens": noise(seeds[9], (TOKENS, D), 1.0, 6.0, ((0, 8), (1, 4))),
        "d_tokens": noise(seeds[10], (TOKENS, D), 1.0, 6.0, ((0, 8), (1, 4))),
    }


def one_head(pieces):
    query_h, tangent_q, key_h, value_h, tangent_k, tangent_v = pieces
    factor = 1.0 / math.sqrt(HD)
    scores = jnp.dot(query_h, key_h.T, preferred_element_type=jnp.float32) * factor
    d_scores = (jnp.dot(tangent_q, key_h.T, preferred_element_type=jnp.float32) + jnp.dot(query_h, tangent_k.T, preferred_element_type=jnp.float32)) * factor
    peak = lax.optimization_barrier(jnp.max(scores, axis=1, keepdims=True))
    weights = jnp.exp(scores - peak)
    totals = lax.optimization_barrier(jnp.sum(weights, axis=1, keepdims=True))
    product = weights * d_scores
    slopes = lax.optimization_barrier(jnp.sum(product, axis=1, keepdims=True))
    weights_b = weights.astype(jnp.bfloat16)
    product_b = product.astype(jnp.bfloat16)
    primal = jnp.dot(weights_b, value_h, preferred_element_type=jnp.float32)
    tangent = jnp.dot(product_b, value_h, preferred_element_type=jnp.float32) + jnp.dot(weights_b, tangent_v, preferred_element_type=jnp.float32)
    outputs = primal / totals
    d_outputs = tangent / totals - slopes / totals * outputs
    return (outputs.astype(jnp.bfloat16), d_outputs.astype(jnp.bfloat16))

def reference(queries, d_queries, key_rows, value_rows, d_key_rows, d_value_rows, live_flags, out_weight, gate_scale, tokens, d_tokens):
    live_rows = live_flags[:, None] > 0

    def masked(matrix):
        return jnp.where(live_rows, matrix, jnp.zeros_like(matrix))

    def by_heads(matrix):
        return matrix.reshape(TOKENS, HEADS, HD).transpose(1, 0, 2)
    stacked = tuple((by_heads(matrix) for matrix in (queries, masked(d_queries), key_rows, value_rows, masked(d_key_rows), masked(d_value_rows))))
    outputs, d_outputs = lax.map(one_head, stacked)

    def regroup(heads_out):
        return heads_out.transpose(1, 0, 2).reshape(TOKENS, N_MP, H_DEV * HD).transpose(1, 0, 2)
    weight_groups = out_weight.reshape(N_MP, H_DEV * HD, D)

    def add_group(running, pieces):
        group_o, group_do, group_w = pieces
        part_y = jnp.dot(group_o, group_w, preferred_element_type=jnp.float32)
        part_dy = jnp.dot(group_do, group_w, preferred_element_type=jnp.float32)
        rounded = lax.optimization_barrier((part_y.astype(jnp.bfloat16), part_dy.astype(jnp.bfloat16)))
        return ((running[0] + rounded[0].astype(jnp.float32), running[1] + rounded[1].astype(jnp.float32)), None)
    blank_sum = jnp.zeros((TOKENS, D), jnp.float32)
    sums, unused = lax.scan(add_group, (blank_sum, blank_sum), (regroup(outputs), regroup(d_outputs), weight_groups))
    result = (tokens.astype(jnp.float32) + gate_scale * sums[0]).astype(jnp.bfloat16)
    d_result = (masked(d_tokens).astype(jnp.float32) + gate_scale * sums[1]).astype(jnp.bfloat16)
    return (result, d_result)
```

```python
import functools
import math

import jax
import jax.numpy as jnp
from jax import lax
from jax.experimental import pallas as pl
from jax.experimental.pallas import tpu as pltpu
from jax.sharding import PartitionSpec as P

HD = 128
FRAME = 32
MESH = pl.DeviceIdType.MESH
F32 = jnp.float32
BF16 = jnp.bfloat16


def ring_place(t, n):
    return jnp.where(t % 2 == 0, t // 2, n - 1 - t // 2)


def ring_member(r, n):
    return jnp.where(r < n // 2, 2 * r, 2 * (n - 1 - r) + 1)


def flipped(me, j):
    other = me
    bit = 1
    while bit <= j:
        if j & bit:
            other = other + bit * (1 - 2 * ((me // bit) % 2))
        bit *= 2
    return other


def dot_nt(a, b):
    return lax.dot_general(a, b, (((1,), (1,)), ((), ())), preferred_element_type=F32)


def dot_nn(a, b):
    return lax.dot_general(a, b, (((1,), (0,)), ((), ())), preferred_element_type=F32)


def fused(
    n,
    n_mp,
    move_w,
    q_hbm,
    dq_hbm,
    k_hbm,
    v_hbm,
    dk_hbm,
    dv_hbm,
    flags,
    w_hbm,
    gate,
    x_hbm,
    dx_hbm,
    out,
    d_out,
    own,
    qcat,
    tkv,
    kv,
    opp,
    m_s,
    l_s,
    c_s,
    a_s,
    g_s,
    ao,
    wbuf,
    acc,
    xbuf,
    own_sem,
    x_sem,
    w_local,
    ks,
    kr,
    ws,
    wr,
    as_,
    ar,
):
    rows, width = q_hbm.shape
    heads = width // HD
    cols = out.shape[1]
    half = n // 2
    t = lax.axis_index("tm")
    m = lax.axis_index("mp")
    place = ring_place(t, n)
    right = ring_member((place + 1) % n, n)
    left = ring_member((place + n - 1) % n, n)
    peers = [flipped(m, j) for j in range(n_mp)]
    factor = 1.0 / math.sqrt(HD)

    def lanes(h):
        return slice(h * HD, (h + 1) * HD)

    loads = [
        pltpu.make_async_copy(src, own.at[i], own_sem.at[i])
        for i, src in enumerate((k_hbm, v_hbm, dk_hbm, dv_hbm, q_hbm, dq_hbm))
    ]
    for load in loads:
        load.start()

    barrier = pltpu.get_barrier_semaphore()
    for dev in [(right, m), (left, m)] + [(t, peers[j]) for j in range(1, n_mp)]:
        pl.semaphore_signal(barrier, inc=1, device_id=dev, device_id_type=MESH)
    pl.semaphore_wait(barrier, 1 + n_mp)

    def exists(d, s, p):
        return s < half or (s == half and (p < 2) == (d == 0))

    def kv_copy(h, d, s, p):
        side = slice(d * rows, (d + 1) * rows)
        if s > 1:
            src = kv.at[h, s - 2, p, side]
        elif p < 2:
            src = (k_hbm, v_hbm)[p].at[:, lanes(h)]
        else:
            src = tkv.at[h, p - 2]
        dst = kv.at[h, s - 1, p, side] if s < half else opp.at[h, p]
        return pltpu.make_async_remote_copy(
            src_ref=src,
            dst_ref=dst,
            send_sem=ks.at[h, d, s - 1, p],
            recv_sem=kr.at[h, d, s - 1, p],
            device_id=((right, left)[d], m),
            device_id_type=MESH,
        )

    def send_own(h, pieces):
        for p in pieces:
            for d in (0, 1):
                kv_copy(h, d, 1, p).start()

    def w_copy(h, j):
        span = pl.ds(pl.multiple_of(peers[j] * cols, HD), cols)
        part = slice(h * HD, (h + 1) * HD)
        if j == 0:
            return pltpu.make_async_copy(
                w_hbm.at[part, span], wbuf.at[0, part], w_local.at[h]
            )
        return pltpu.make_async_remote_copy(
            src_ref=w_hbm.at[part, span],
            dst_ref=wbuf.at[j, part],
            send_sem=ws.at[h, j],
            recv_sem=wr.at[h, j],
            device_id=(t, peers[j]),
            device_id_type=MESH,
        )

    def ao_copy(h, j):
        relay = j % 2 == 1 and j > 1
        return pltpu.make_async_remote_copy(
            src_ref=ao.at[h, j - 1 if relay else 0],
            dst_ref=ao.at[h, j],
            send_sem=as_.at[h, j],
            recv_sem=ar.at[h, j],
            device_id=(t, peers[1] if relay else peers[j]),
            device_id_type=MESH,
        )

    send_own(0, (0, 1))
    if move_w:
        for h in range(heads):
            for j in list(range(2, n_mp)) + [1, 0]:
                w_copy(h, j).start()
    x_loads = [
        pltpu.make_async_copy(src, xbuf.at[i], x_sem.at[i])
        for i, src in enumerate((x_hbm, dx_hbm))
    ]
    for load in x_loads:
        load.start()
    for load in loads:
        load.wait()

    live = [
        jnp.where(flags[i * FRAME] > 0, 1.0, 0.0).astype(F32)
        for i in range(rows // FRAME)
    ]

    def masked(value, i):
        scale = jnp.full(value.shape, live[i], F32)
        return (value.astype(F32) * scale).astype(BF16)

    for h in range(heads):
        for i in range(rows // FRAME):
            part = slice(i * FRAME, (i + 1) * FRAME)
            tkv[h, 0, part] = masked(own[2, part, lanes(h)], i)
            tkv[h, 1, part] = masked(own[3, part, lanes(h)], i)
        if h == 0:
            send_own(0, (2, 3))
    for h in range(heads):
        for i in range(rows // FRAME):
            part = slice(i * FRAME, (i + 1) * FRAME)
            qcat[h, part, 0:HD] = masked(own[5, part, lanes(h)], i)
        qcat[h, :, HD : 2 * HD] = own[4, :, lanes(h)]

    def attend(h, k, v, tk, tv, first):
        queries = qcat[h, :, HD : 2 * HD]
        scores = dot_nt(queries, k)
        d_scores = dot_nt(qcat[h], jnp.concatenate([k, tk], axis=1)) * factor
        peak = jnp.max(scores, axis=1, keepdims=True)
        if not first:
            peak_old = m_s[...]
            peak = jnp.maximum(peak_old, peak)
            rescale = jnp.exp((peak_old - peak) * factor)
        weights = jnp.exp((scores - peak) * factor)
        product = weights * d_scores
        total = jnp.sum(weights, axis=1, keepdims=True)
        slope = jnp.sum(product, axis=1, keepdims=True)
        weights_b = weights.astype(BF16)
        product_b = product.astype(BF16)
        primal = dot_nn(weights_b, v)
        tangent = dot_nn(product_b, v) + dot_nn(weights_b, tv)
        m_s[...] = peak
        if first:
            l_s[...] = total
            c_s[...] = slope
            a_s[...] = primal
            g_s[...] = tangent
        else:
            l_s[...] = l_s[...] * rescale + total
            c_s[...] = c_s[...] * rescale + slope
            a_s[...] = a_s[...] * rescale + primal
            g_s[...] = g_s[...] * rescale + tangent

    def finish(h):
        inverse = 1.0 / l_s[...]
        outputs = a_s[...] * inverse
        d_outputs = g_s[...] * inverse - (c_s[...] * inverse) * outputs
        ao[h, 0, 0:rows] = outputs.astype(BF16)
        ao[h, 0, rows : 2 * rows] = d_outputs.astype(BF16)
        for j in list(range(2, n_mp, 2)) + [1]:
            ao_copy(h, j).start()

    def relay(h):
        for j in range(2, n_mp, 2):
            ao_copy(h, j).wait_recv()
            ao_copy(h, j + 1).start()

    for h in range(heads):
        attend(h, own[0, :, lanes(h)], own[1, :, lanes(h)], tkv[h, 0], tkv[h, 1], True)
        for s in range(1, half):
            for p in range(4):
                for d in (0, 1):
                    kv_copy(h, d, s, p).wait_recv()
                    if exists(d, s + 1, p):
                        kv_copy(h, d, s + 1, p).start()
            if h + 1 < heads:
                if s == 1:
                    send_own(h + 1, (0, 1))
                if s == min(2, half - 1):
                    send_own(h + 1, (2, 3))
            attend(h, *[kv[h, s - 1, p] for p in range(4)], False)
        if h > 0:
            relay(h - 1)
        for p in range(4):
            kv_copy(h, 0 if p < 2 else 1, half, p).wait_recv()
        attend(h, *[opp[h, p] for p in range(4)], False)
        finish(h)

    step = 2 * HD if cols % (2 * HD) == 0 else cols
    chunks = [slice(c, c + step) for c in range(0, cols, step)]

    def w_part(h, j, chunk):
        part = slice(h * HD, (h + 1) * HD)
        if move_w:
            return wbuf[j, part, chunk]
        return w_hbm[peers[j], part, chunk]

    def project(h, slots, chunk):
        attn = jnp.concatenate([ao[h, j] for j in slots], axis=1)
        weight = jnp.concatenate([w_part(h, j, chunk) for j in slots], axis=0)
        return dot_nn(attn, weight)

    near = (0, 1)
    far = tuple(range(2, n_mp))
    last = heads - 1
    for h in range(last):
        for j in range(1, n_mp):
            if j % 2 == 1:
                ao_copy(h, j).wait_recv()
            if move_w:
                w_copy(h, j).wait_recv()
        if move_w:
            w_copy(h, 0).wait()
        for chunk in chunks:
            part = project(h, near + far, chunk)
            acc[:, chunk] = part if h == 0 else acc[:, chunk] + part
    ao_copy(last, 1).wait_recv()
    if move_w:
        w_copy(last, 0).wait()
        for j in range(1, n_mp):
            w_copy(last, j).wait_recv()
    for chunk in chunks:
        part = project(last, near, chunk)
        acc[:, chunk] = part if last == 0 else acc[:, chunk] + part
    for load in x_loads:
        load.wait()
    relay(last)
    for j in range(3, n_mp, 2):
        ao_copy(last, j).wait_recv()
    for chunk in chunks:
        part = acc[:, chunk] + project(last, far, chunk)
        scale = gate[:, chunk]
        out[:, chunk] = (xbuf[0, :, chunk].astype(F32) + scale * part[0:rows]).astype(BF16)
        for i in range(rows // FRAME):
            piece = slice(i * FRAME, (i + 1) * FRAME)
            base = xbuf[1, piece, chunk].astype(F32)
            base = base * jnp.full(base.shape, live[i], F32)
            delta = part[rows + i * FRAME : rows + (i + 1) * FRAME]
            d_out[piece, chunk] = (base + scale * delta).astype(BF16)

    for h in range(heads):
        for s in range(1, half + 1):
            for p in range(4):
                for d in (0, 1):
                    if exists(d, s, p):
                        kv_copy(h, d, s, p).wait_send()
        for j in range(1, n_mp):
            ao_copy(h, j).wait_send()
            if move_w:
                w_copy(h, j).wait_send()


def per_device(n, n_mp, q, dq, k, v, dk, dv, flags, w, gate, x, dx):
    rows, width = q.shape
    cols = x.shape[1]
    heads = width // HD
    half = n // 2
    move_w = cols % HD == 0
    if not move_w:
        w = lax.all_to_all(w, "mp", split_axis=1, concat_axis=0, tiled=True)
        w = w.reshape(n_mp, width, cols)
    anywhere = pl.BlockSpec(memory_space=pl.ANY)
    vmem = pl.BlockSpec(memory_space=pltpu.VMEM)
    dma = pltpu.SemaphoreType.DMA
    return pl.pallas_call(
        functools.partial(fused, n, n_mp, move_w),
        out_shape=(jax.ShapeDtypeStruct(x.shape, BF16), jax.ShapeDtypeStruct(x.shape, BF16)),
        in_specs=[anywhere] * 6
        + [pl.BlockSpec(memory_space=pltpu.SMEM), anywhere if move_w else vmem, vmem]
        + [anywhere] * 2,
        out_specs=(vmem, vmem),
        scratch_shapes=[
            pltpu.VMEM((6, rows, width), BF16),
            pltpu.VMEM((heads, rows, 2 * HD), BF16),
            pltpu.VMEM((heads, 2, rows, HD), BF16),
            pltpu.VMEM((heads, half - 1, 4, 2 * rows, HD), BF16),
            pltpu.VMEM((heads, 4, rows, HD), BF16),
            pltpu.VMEM((rows, 1), F32),
            pltpu.VMEM((rows, 1), F32),
            pltpu.VMEM((rows, 1), F32),
            pltpu.VMEM((rows, HD), F32),
            pltpu.VMEM((rows, HD), F32),
            pltpu.VMEM((heads, n_mp, 2 * rows, HD), BF16),
            pltpu.VMEM((n_mp, width, cols) if move_w else (1, 16, HD), BF16),
            pltpu.VMEM((2 * rows, cols), F32),
            pltpu.VMEM((2, rows, cols), BF16),
            dma((6,)),
            dma((2,)),
            dma((heads,)),
            dma((heads, 2, half, 4)),
            dma((heads, 2, half, 4)),
            dma((heads, n_mp)),
            dma((heads, n_mp)),
            dma((heads, n_mp)),
            dma((heads, n_mp)),
        ],
        compiler_params=pltpu.CompilerParams(
            collective_id=0, has_side_effects=True, vmem_limit_bytes=48 * 1024 * 1024
        ),
    )(q, dq, k, v, dk, dv, flags, w, gate.reshape(1, cols), x, dx)


def solution(mesh):
    both = P("tm", "mp")
    placed = (both,) * 6 + (P("tm"), P("mp", None), P("mp"), both, both)
    return jax.shard_map(
        functools.partial(per_device, mesh.shape["tm"], mesh.shape["mp"]),
        mesh=mesh,
        in_specs=placed,
        out_specs=(both, both),
        check_vma=False,
    )
```

```python
import functools
import math

import jax
import jax.numpy as jnp
from jax import lax
from jax.experimental import pallas as pl
from jax.experimental.pallas import tpu as pltpu
from jax.sharding import PartitionSpec as P

HD = 128
FRAME = 32
MESH = pl.DeviceIdType.MESH
F32 = jnp.float32
BF16 = jnp.bfloat16


def ring_place(t, n):
    return jnp.where(t % 2 == 0, t // 2, n - 1 - t // 2)


def ring_member(r, n):
    return jnp.where(r < n // 2, 2 * r, 2 * (n - 1 - r) + 1)


def flipped(me, j):
    other = me
    bit = 1
    while bit <= j:
        if j & bit:
            other = other + bit * (1 - 2 * ((me // bit) % 2))
        bit *= 2
    return other


def dot_nt(a, b):
    return lax.dot_general(a, b, (((1,), (1,)), ((), ())), preferred_element_type=F32)


def dot_nn(a, b):
    return lax.dot_general(a, b, (((1,), (0,)), ((), ())), preferred_element_type=F32)


def fused(
    n,
    n_mp,
    move_w,
    q_hbm,
    dq_hbm,
    k_hbm,
    v_hbm,
    dk_hbm,
    dv_hbm,
    flags,
    w_hbm,
    gate,
    x_hbm,
    dx_hbm,
    out,
    d_out,
    own,
    qcat,
    tkv,
    kv,
    opp,
    m_s,
    l_s,
    c_s,
    a_s,
    g_s,
    ao,
    wbuf,
    acc,
    xbuf,
    own_sem,
    x_sem,
    w_local,
    ks,
    kr,
    ws,
    wr,
    as_,
    ar,
):
    rows, width = q_hbm.shape
    heads = width // HD
    cols = out.shape[1]
    half = n // 2
    t = lax.axis_index("tm")
    m = lax.axis_index("mp")
    place = ring_place(t, n)
    right = ring_member((place + 1) % n, n)
    left = ring_member((place + n - 1) % n, n)
    peers = [flipped(m, j) for j in range(n_mp)]
    factor = 1.0 / math.sqrt(HD)

    def lanes(h):
        return slice(h * HD, (h + 1) * HD)

    loads = [
        pltpu.make_async_copy(src, own.at[i], own_sem.at[i])
        for i, src in enumerate((k_hbm, v_hbm, dk_hbm, dv_hbm, q_hbm, dq_hbm))
    ]
    for load in loads:
        load.start()

    barrier = pltpu.get_barrier_semaphore()
    for dev in [(right, m), (left, m)] + [(t, peers[j]) for j in range(1, n_mp)]:
        pl.semaphore_signal(barrier, inc=1, device_id=dev, device_id_type=MESH)
    pl.semaphore_wait(barrier, 1 + n_mp)

    def exists(d, s, p):
        return s < half or (s == half and (p < 2) == (d == 0))

    def kv_copy(h, d, s, p):
        side = slice(d * rows, (d + 1) * rows)
        if s > 1:
            src = kv.at[h, s - 2, p, side]
        elif p < 2:
            src = (k_hbm, v_hbm)[p].at[:, lanes(h)]
        else:
            src = tkv.at[h, p - 2]
        dst = kv.at[h, s - 1, p, side] if s < half else opp.at[h, p]
        return pltpu.make_async_remote_copy(
            src_ref=src,
            dst_ref=dst,
            send_sem=ks.at[h, d, s - 1, p],
            recv_sem=kr.at[h, d, s - 1, p],
            device_id=((right, left)[d], m),
            device_id_type=MESH,
        )

    def send_own(h, pieces):
        for p in pieces:
            for d in (0, 1):
                kv_copy(h, d, 1, p).start()

    def w_copy(h, j):
        span = pl.ds(pl.multiple_of(peers[j] * cols, HD), cols)
        part = slice(h * HD, (h + 1) * HD)
        if j == 0:
            return pltpu.make_async_copy(
                w_hbm.at[part, span], wbuf.at[0, part], w_local.at[h]
            )
        return pltpu.make_async_remote_copy(
            src_ref=w_hbm.at[part, span],
            dst_ref=wbuf.at[j, part],
            send_sem=ws.at[h, j],
            recv_sem=wr.at[h, j],
            device_id=(t, peers[j]),
            device_id_type=MESH,
        )

    def ao_copy(h, j):
        relay = j % 2 == 1 and j > 1
        return pltpu.make_async_remote_copy(
            src_ref=ao.at[h, j - 1 if relay else 0],
            dst_ref=ao.at[h, j],
            send_sem=as_.at[h, j],
            recv_sem=ar.at[h, j],
            device_id=(t, peers[1] if relay else peers[j]),
            device_id_type=MESH,
        )

    send_own(0, (0, 1))
    if move_w:
        for h in range(heads):
            for j in list(range(2, n_mp)) + [1, 0]:
                w_copy(h, j).start()
    x_loads = [
        pltpu.make_async_copy(src, xbuf.at[i], x_sem.at[i])
        for i, src in enumerate((x_hbm, dx_hbm))
    ]
    for load in x_loads:
        load.start()
    for load in loads:
        load.wait()

    live = [
        jnp.where(flags[i * FRAME] > 0, 1.0, 0.0).astype(F32)
        for i in range(rows // FRAME)
    ]

    def masked(value, i):
        scale = jnp.full(value.shape, live[i], F32)
        return (value.astype(F32) * scale).astype(BF16)

    for h in range(heads):
        for i in range(rows // FRAME):
            part = slice(i * FRAME, (i + 1) * FRAME)
            tkv[h, 0, part] = masked(own[2, part, lanes(h)], i)
            tkv[h, 1, part] = masked(own[3, part, lanes(h)], i)
        if h == 0:
            send_own(0, (2, 3))
    for h in range(heads):
        for i in range(rows // FRAME):
            part = slice(i * FRAME, (i + 1) * FRAME)
            qcat[h, part, 0:HD] = masked(own[5, part, lanes(h)], i)
        qcat[h, :, HD : 2 * HD] = own[4, :, lanes(h)]

    def attend(h, k, v, tk, tv, first):
        queries = qcat[h, :, HD : 2 * HD]
        scores = dot_nt(queries, k)
        d_scores = dot_nt(qcat[h], jnp.concatenate([k, tk], axis=1)) * factor
        peak = jnp.max(scores, axis=1, keepdims=True)
        if not first:
            peak_old = m_s[...]
            peak = jnp.maximum(peak_old, peak)
            rescale = jnp.exp((peak_old - peak) * factor)
        weights = jnp.exp((scores - peak) * factor)
        product = weights * d_scores
        total = jnp.sum(weights, axis=1, keepdims=True)
        slope = jnp.sum(product, axis=1, keepdims=True)
        weights_b = weights.astype(BF16)
        product_b = product.astype(BF16)
        primal = dot_nn(weights_b, v)
        tangent = dot_nn(product_b, v) + dot_nn(weights_b, tv)
        m_s[...] = peak
        if first:
            l_s[...] = total
            c_s[...] = slope
            a_s[...] = primal
            g_s[...] = tangent
        else:
            l_s[...] = l_s[...] * rescale + total
            c_s[...] = c_s[...] * rescale + slope
            a_s[...] = a_s[...] * rescale + primal
            g_s[...] = g_s[...] * rescale + tangent

    def finish(h):
        inverse = 1.0 / l_s[...]
        outputs = a_s[...] * inverse
        d_outputs = g_s[...] * inverse - (c_s[...] * inverse) * outputs
        ao[h, 0, 0:rows] = outputs.astype(BF16)
        ao[h, 0, rows : 2 * rows] = d_outputs.astype(BF16)
        for j in list(range(2, n_mp, 2)) + [1]:
            ao_copy(h, j).start()

    def relay(h):
        for j in range(2, n_mp, 2):
            ao_copy(h, j).wait_recv()
            ao_copy(h, j + 1).start()

    for h in range(heads):
        attend(h, own[0, :, lanes(h)], own[1, :, lanes(h)], tkv[h, 0], tkv[h, 1], True)
        for s in range(1, half):
            for p in range(4):
                for d in (0, 1):
                    kv_copy(h, d, s, p).wait_recv()
                    if exists(d, s + 1, p):
                        kv_copy(h, d, s + 1, p).start()
            if h + 1 < heads:
                if s == 1:
                    send_own(h + 1, (0, 1))
                if s == min(2, half - 1):
                    send_own(h + 1, (2, 3))
            attend(h, *[kv[h, s - 1, p] for p in range(4)], False)
        if h > 0:
            relay(h - 1)
        for p in range(4):
            kv_copy(h, 0 if p < 2 else 1, half, p).wait_recv()
        attend(h, *[opp[h, p] for p in range(4)], False)
        finish(h)

    step = 2 * HD if cols % (2 * HD) == 0 else cols
    chunks = [slice(c, c + step) for c in range(0, cols, step)]

    def w_part(h, j, chunk):
        part = slice(h * HD, (h + 1) * HD)
        if move_w:
            return wbuf[j, part, chunk]
        return w_hbm[peers[j], part, chunk]

    def project(h, slots, chunk):
        attn = jnp.concatenate([ao[h, j] for j in slots], axis=1)
        weight = jnp.concatenate([w_part(h, j, chunk) for j in slots], axis=0)
        return dot_nn(attn, weight)

    near = (0, 1)
    far = tuple(range(2, n_mp))
    last = heads - 1
    for h in range(last):
        for j in range(1, n_mp):
            if j % 2 == 1:
                ao_copy(h, j).wait_recv()
            if move_w:
                w_copy(h, j).wait_recv()
        if move_w:
            w_copy(h, 0).wait()
        for chunk in chunks:
            part = project(h, near + far, chunk)
            acc[:, chunk] = part if h == 0 else acc[:, chunk] + part
    ao_copy(last, 1).wait_recv()
    if move_w:
        w_copy(last, 0).wait()
        for j in range(1, n_mp):
            w_copy(last, j).wait_recv()
    for chunk in chunks:
        part = project(last, near, chunk)
        acc[:, chunk] = part if last == 0 else acc[:, chunk] + part
    for load in x_loads:
        load.wait()
    relay(last)
    for j in range(3, n_mp, 2):
        ao_copy(last, j).wait_recv()
    for chunk in chunks:
        part = acc[:, chunk] + project(last, far, chunk)
        scale = gate[:, chunk]
        out[:, chunk] = (xbuf[0, :, chunk].astype(F32) + scale * part[0:rows]).astype(BF16)
        for i in range(rows // FRAME):
            piece = slice(i * FRAME, (i + 1) * FRAME)
            base = xbuf[1, piece, chunk].astype(F32)
            base = base * jnp.full(base.shape, live[i], F32)
            delta = part[rows + i * FRAME : rows + (i + 1) * FRAME]
            d_out[piece, chunk] = (base + scale * delta).astype(BF16)

    for h in range(heads):
        for s in range(1, half + 1):
            for p in range(4):
                for d in (0, 1):
                    if exists(d, s, p):
                        kv_copy(h, d, s, p).wait_send()
        for j in range(1, n_mp):
            ao_copy(h, j).wait_send()
            if move_w:
                w_copy(h, j).wait_send()


def per_device(n, n_mp, q, dq, k, v, dk, dv, flags, w, gate, x, dx):
    rows, width = q.shape
    cols = x.shape[1]
    heads = width // HD
    half = n // 2
    move_w = cols % HD == 0
    if not move_w:
        w = lax.all_to_all(w, "mp", split_axis=1, concat_axis=0, tiled=True)
        w = w.reshape(n_mp, width, cols)
    anywhere = pl.BlockSpec(memory_space=pl.ANY)
    vmem = pl.BlockSpec(memory_space=pltpu.VMEM)
    dma = pltpu.SemaphoreType.DMA
    return pl.pallas_call(
        functools.partial(fused, n, n_mp, move_w),
        out_shape=(jax.ShapeDtypeStruct(x.shape, BF16), jax.ShapeDtypeStruct(x.shape, BF16)),
        in_specs=[anywhere] * 6
        + [pl.BlockSpec(memory_space=pltpu.SMEM), anywhere if move_w else vmem, vmem]
        + [anywhere] * 2,
        out_specs=(vmem, vmem),
        scratch_shapes=[
            pltpu.VMEM((6, rows, width), BF16),
            pltpu.VMEM((heads, rows, 2 * HD), BF16),
            pltpu.VMEM((heads, 2, rows, HD), BF16),
            pltpu.VMEM((heads, half - 1, 4, 2 * rows, HD), BF16),
            pltpu.VMEM((heads, 4, rows, HD), BF16),
            pltpu.VMEM((rows, 1), F32),
            pltpu.VMEM((rows, 1), F32),
            pltpu.VMEM((rows, 1), F32),
            pltpu.VMEM((rows, HD), F32),
            pltpu.VMEM((rows, HD), F32),
            pltpu.VMEM((heads, n_mp, 2 * rows, HD), BF16),
            pltpu.VMEM((n_mp, width, cols) if move_w else (1, 16, HD), BF16),
            pltpu.VMEM((2 * rows, cols), F32),
            pltpu.VMEM((2, rows, cols), BF16),
            dma((6,)),
            dma((2,)),
            dma((heads,)),
            dma((heads, 2, half, 4)),
            dma((heads, 2, half, 4)),
            dma((heads, n_mp)),
            dma((heads, n_mp)),
            dma((heads, n_mp)),
            dma((heads, n_mp)),
        ],
        compiler_params=pltpu.CompilerParams(
            collective_id=0, has_side_effects=True, vmem_limit_bytes=67043328
        ),
    )(q, dq, k, v, dk, dv, flags, w, gate.reshape(1, cols), x, dx)


def solution(mesh):
    both = P("tm", "mp")
    placed = (both,) * 6 + (P("tm"), P("mp", None), P("mp"), both, both)
    return jax.shard_map(
        functools.partial(per_device, mesh.shape["tm"], mesh.shape["mp"]),
        mesh=mesh,
        in_specs=placed,
        out_specs=(both, both),
        check_vma=False,
    )
```

```python
import functools
import math

import jax
import jax.numpy as jnp
from jax import lax
from jax.experimental import pallas as pl
from jax.experimental.pallas import tpu as pltpu
from jax.sharding import PartitionSpec as P

HD = 128
FRAME = 32
MESH = pl.DeviceIdType.MESH
F32 = jnp.float32
BF16 = jnp.bfloat16


def ring_place(t, n):
    return jnp.where(t % 2 == 0, t // 2, n - 1 - t // 2)


def ring_member(r, n):
    return jnp.where(r < n // 2, 2 * r, 2 * (n - 1 - r) + 1)


def flipped(me, j):
    other = me
    bit = 1
    while bit <= j:
        if j & bit:
            other = other + bit * (1 - 2 * ((me // bit) % 2))
        bit *= 2
    return other


def dot_nt(a, b):
    return lax.dot_general(a, b, (((1,), (1,)), ((), ())), preferred_element_type=F32)


def dot_nn(a, b):
    return lax.dot_general(a, b, (((1,), (0,)), ((), ())), preferred_element_type=F32)


def fused(
    n,
    n_mp,
    move_w,
    q_hbm,
    dq_hbm,
    k_hbm,
    v_hbm,
    dk_hbm,
    dv_hbm,
    flags,
    w_hbm,
    gate,
    x_hbm,
    dx_hbm,
    out,
    d_out,
    own,
    qcat,
    tkv,
    kv,
    opp,
    m_s,
    l_s,
    c_s,
    a_s,
    g_s,
    ao,
    wbuf,
    acc,
    xbuf,
    own_sem,
    x_sem,
    w_local,
    ks,
    kr,
    ws,
    wr,
    as_,
    ar,
):
    rows, width = q_hbm.shape
    heads = width // HD
    cols = out.shape[1]
    half = n // 2
    t = lax.axis_index("tm")
    m = lax.axis_index("mp")
    place = ring_place(t, n)
    right = ring_member((place + 1) % n, n)
    left = ring_member((place + n - 1) % n, n)
    peers = [flipped(m, j) for j in range(n_mp)]
    factor = 1.0 / math.sqrt(HD)

    def lanes(h):
        return slice(h * HD, (h + 1) * HD)

    loads = [
        pltpu.make_async_copy(src, own.at[i], own_sem.at[i])
        for i, src in enumerate((k_hbm, v_hbm, dk_hbm, dv_hbm, q_hbm, dq_hbm))
    ]
    for load in loads:
        load.start()

    barrier = pltpu.get_barrier_semaphore()
    for dev in [(right, m), (left, m)] + [(t, peers[j]) for j in range(1, n_mp)]:
        pl.semaphore_signal(barrier, inc=1, device_id=dev, device_id_type=MESH)
    pl.semaphore_wait(barrier, 1 + n_mp)

    def exists(d, s, p):
        return s < half or (s == half and (p < 2) == (d == 0))

    def kv_copy(h, d, s, p):
        side = slice(d * rows, (d + 1) * rows)
        if s > 1:
            src = kv.at[h, s - 2, p, side]
        elif p < 2:
            src = (k_hbm, v_hbm)[p].at[:, lanes(h)]
        else:
            src = tkv.at[h, p - 2]
        dst = kv.at[h, s - 1, p, side] if s < half else opp.at[h, p]
        return pltpu.make_async_remote_copy(
            src_ref=src,
            dst_ref=dst,
            send_sem=ks.at[h, d, s - 1, p],
            recv_sem=kr.at[h, d, s - 1, p],
            device_id=((right, left)[d], m),
            device_id_type=MESH,
        )

    def send_own(h, pieces):
        for p in pieces:
            for d in (0, 1):
                kv_copy(h, d, 1, p).start()

    def w_copy(h, j):
        span = pl.ds(pl.multiple_of(peers[j] * cols, HD), cols)
        part = slice(h * HD, (h + 1) * HD)
        if j == 0:
            return pltpu.make_async_copy(
                w_hbm.at[part, span], wbuf.at[0, part], w_local.at[h]
            )
        return pltpu.make_async_remote_copy(
            src_ref=w_hbm.at[part, span],
            dst_ref=wbuf.at[j, part],
            send_sem=ws.at[h, j],
            recv_sem=wr.at[h, j],
            device_id=(t, peers[j]),
            device_id_type=MESH,
        )

    def ao_copy(h, j):
        relay = j % 2 == 1 and j > 1
        return pltpu.make_async_remote_copy(
            src_ref=ao.at[h, j - 1 if relay else 0],
            dst_ref=ao.at[h, j],
            send_sem=as_.at[h, j],
            recv_sem=ar.at[h, j],
            device_id=(t, peers[1] if relay else peers[j]),
            device_id_type=MESH,
        )

    send_own(0, (0, 1))
    if move_w:
        for h in range(heads):
            for j in list(range(2, n_mp)) + [1, 0]:
                w_copy(h, j).start()
    x_loads = [
        pltpu.make_async_copy(src, xbuf.at[i], x_sem.at[i])
        for i, src in enumerate((x_hbm, dx_hbm))
    ]
    for load in x_loads:
        load.start()
    for load in loads:
        load.wait()

    live = [
        jnp.where(flags[i * FRAME] > 0, 1.0, 0.0).astype(F32)
        for i in range(rows // FRAME)
    ]

    def masked(value, i):
        scale = jnp.full(value.shape, live[i], F32)
        return (value.astype(F32) * scale).astype(BF16)

    for h in range(heads):
        for i in range(rows // FRAME):
            part = slice(i * FRAME, (i + 1) * FRAME)
            tkv[h, 0, part] = masked(own[2, part, lanes(h)], i)
            tkv[h, 1, part] = masked(own[3, part, lanes(h)], i)
        if h == 0:
            send_own(0, (2, 3))
            for g in range(1, heads):
                send_own(g, (0, 1))
        else:
            send_own(h, (2, 3))
    for h in range(heads):
        for i in range(rows // FRAME):
            part = slice(i * FRAME, (i + 1) * FRAME)
            qcat[h, part, 0:HD] = masked(own[5, part, lanes(h)], i)
        qcat[h, :, HD : 2 * HD] = own[4, :, lanes(h)]

    def attend(h, k, v, tk, tv, first):
        queries = qcat[h, :, HD : 2 * HD]
        scores = dot_nt(queries, k)
        d_scores = dot_nt(qcat[h], jnp.concatenate([k, tk], axis=1)) * factor
        peak = jnp.max(scores, axis=1, keepdims=True)
        if not first:
            peak_old = m_s[h]
            peak = jnp.maximum(peak_old, peak)
            rescale = jnp.exp((peak_old - peak) * factor)
        weights = jnp.exp((scores - peak) * factor)
        product = weights * d_scores
        total = jnp.sum(weights, axis=1, keepdims=True)
        slope = jnp.sum(product, axis=1, keepdims=True)
        weights_b = weights.astype(BF16)
        product_b = product.astype(BF16)
        primal = dot_nn(weights_b, v)
        tangent = dot_nn(product_b, v) + dot_nn(weights_b, tv)
        m_s[h] = peak
        if first:
            l_s[h] = total
            c_s[h] = slope
            a_s[h] = primal
            g_s[h] = tangent
        else:
            l_s[h] = l_s[h] * rescale + total
            c_s[h] = c_s[h] * rescale + slope
            a_s[h] = a_s[h] * rescale + primal
            g_s[h] = g_s[h] * rescale + tangent

    def finish(h):
        inverse = 1.0 / l_s[h]
        outputs = a_s[h] * inverse
        d_outputs = g_s[h] * inverse - (c_s[h] * inverse) * outputs
        ao[h, 0, 0:rows] = outputs.astype(BF16)
        ao[h, 0, rows : 2 * rows] = d_outputs.astype(BF16)
        for j in list(range(2, n_mp, 2)) + [1]:
            ao_copy(h, j).start()

    def relay(h):
        for j in range(2, n_mp, 2):
            ao_copy(h, j).wait_recv()
            ao_copy(h, j + 1).start()

    for h in range(heads):
        attend(h, own[0, :, lanes(h)], own[1, :, lanes(h)], tkv[h, 0], tkv[h, 1], True)
    for s in range(1, half):
        for h in range(heads):
            for p in range(4):
                for d in (0, 1):
                    kv_copy(h, d, s, p).wait_recv()
                    if exists(d, s + 1, p):
                        kv_copy(h, d, s + 1, p).start()
            attend(h, *[kv[h, s - 1, p] for p in range(4)], False)
    for h in range(heads):
        for p in range(4):
            kv_copy(h, 0 if p < 2 else 1, half, p).wait_recv()
        attend(h, *[opp[h, p] for p in range(4)], False)
        finish(h)

    step = 2 * HD if cols % (2 * HD) == 0 else cols
    chunks = [slice(c, c + step) for c in range(0, cols, step)]

    def w_part(h, j, chunk):
        part = slice(h * HD, (h + 1) * HD)
        if move_w:
            return wbuf[j, part, chunk]
        return w_hbm[peers[j], part, chunk]

    def project(slots, chunk):
        attn = jnp.concatenate([ao[h, j] for h, j in slots], axis=1)
        weight = jnp.concatenate([w_part(h, j, chunk) for h, j in slots], axis=0)
        return dot_nn(attn, weight)

    if move_w:
        for h in range(heads):
            w_copy(h, 0).wait()
            for j in range(1, n_mp):
                w_copy(h, j).wait_recv()
    for load in x_loads:
        load.wait()
    last = heads - 1
    for h in range(heads):
        ao_copy(h, 1).wait_recv()
    near = [(h, j) for h in range(heads) for j in (0, 1)]
    for chunk in chunks:
        acc[:, chunk] = project(near, chunk)
    for h in range(last):
        relay(h)
    for h in range(last):
        for j in range(3, n_mp, 2):
            ao_copy(h, j).wait_recv()
    far = [(h, j) for h in range(last) for j in range(2, n_mp)]
    for chunk in chunks:
        acc[:, chunk] += project(far, chunk)
    relay(last)
    even = [(last, j) for j in range(2, n_mp, 2)]
    for chunk in chunks:
        acc[:, chunk] += project(even, chunk)
    for j in range(3, n_mp, 2):
        ao_copy(last, j).wait_recv()
    odd = [(last, j) for j in range(3, n_mp, 2)]
    for chunk in chunks:
        part = acc[:, chunk] + project(odd, chunk)
        scale = gate[chunk].reshape(1, step)
        out[:, chunk] = (xbuf[0, :, chunk].astype(F32) + scale * part[0:rows]).astype(BF16)
        for i in range(rows // FRAME):
            piece = slice(i * FRAME, (i + 1) * FRAME)
            base = xbuf[1, piece, chunk].astype(F32)
            base = base * jnp.full(base.shape, live[i], F32)
            delta = part[rows + i * FRAME : rows + (i + 1) * FRAME]
            d_out[piece, chunk] = (base + scale * delta).astype(BF16)

    for h in range(heads):
        for s in range(1, half + 1):
            for p in range(4):
                for d in (0, 1):
                    if exists(d, s, p):
                        kv_copy(h, d, s, p).wait_send()
        for j in range(1, n_mp):
            ao_copy(h, j).wait_send()
            if move_w:
                w_copy(h, j).wait_send()


def per_device(n, n_mp, q, dq, k, v, dk, dv, flags, w, gate, x, dx):
    rows, width = q.shape
    cols = x.shape[1]
    heads = width // HD
    half = n // 2
    move_w = cols % HD == 0
    if not move_w:
        w = lax.all_to_all(w, "mp", split_axis=1, concat_axis=0, tiled=True)
        w = w.reshape(n_mp, width, cols)
    anywhere = pl.BlockSpec(memory_space=pl.ANY)
    vmem = pl.BlockSpec(memory_space=pltpu.VMEM)
    dma = pltpu.SemaphoreType.DMA
    return pl.pallas_call(
        functools.partial(fused, n, n_mp, move_w),
        out_shape=(pltpu.VMEM(x.shape, BF16), pltpu.VMEM(x.shape, BF16)),
        in_specs=[anywhere] * 6
        + [pl.BlockSpec(memory_space=pltpu.SMEM), anywhere if move_w else vmem, vmem]
        + [anywhere] * 2,
        out_specs=(vmem, vmem),
        scratch_shapes=[
            pltpu.VMEM((6, rows, width), BF16),
            pltpu.VMEM((heads, rows, 2 * HD), BF16),
            pltpu.VMEM((heads, 2, rows, HD), BF16),
            pltpu.VMEM((heads, half - 1, 4, 2 * rows, HD), BF16),
            pltpu.VMEM((heads, 4, rows, HD), BF16),
            pltpu.VMEM((heads, rows, 1), F32),
            pltpu.VMEM((heads, rows, 1), F32),
            pltpu.VMEM((heads, rows, 1), F32),
            pltpu.VMEM((heads, rows, HD), F32),
            pltpu.VMEM((heads, rows, HD), F32),
            pltpu.VMEM((heads, n_mp, 2 * rows, HD), BF16),
            pltpu.VMEM((n_mp, width, cols) if move_w else (1, 16, HD), BF16),
            pltpu.VMEM((2 * rows, cols), F32),
            pltpu.VMEM((2, rows, cols), BF16),
            dma((6,)),
            dma((2,)),
            dma((heads,)),
            dma((heads, 2, half, 4)),
            dma((heads, 2, half, 4)),
            dma((heads, n_mp)),
            dma((heads, n_mp)),
            dma((heads, n_mp)),
            dma((heads, n_mp)),
        ],
        compiler_params=pltpu.CompilerParams(
            collective_id=0, has_side_effects=True, vmem_limit_bytes=65000000
        ),
    )(q, dq, k, v, dk, dv, flags, w, gate, x, dx)


def solution(mesh):
    both = P("tm", "mp")
    placed = (both,) * 6 + (P("tm"), P("mp", None), P("mp"), both, both)
    return jax.shard_map(
        functools.partial(per_device, mesh.shape["tm"], mesh.shape["mp"]),
        mesh=mesh,
        in_specs=placed,
        out_specs=(both, both),
        check_vma=False,
    )
```

```python
import functools
import math

import jax
import jax.numpy as jnp
from jax import lax
from jax.experimental import pallas as pl
from jax.experimental.pallas import tpu as pltpu
from jax.sharding import PartitionSpec as P

HD = 128
FRAME = 32
MESH = pl.DeviceIdType.MESH
F32 = jnp.float32
BF16 = jnp.bfloat16


def ring_place(t, n):
    return jnp.where(t % 2 == 0, t // 2, n - 1 - t // 2)


def ring_member(r, n):
    return jnp.where(r < n // 2, 2 * r, 2 * (n - 1 - r) + 1)


def flipped(me, j):
    other = me
    bit = 1
    while bit <= j:
        if j & bit:
            other = other + bit * (1 - 2 * ((me // bit) % 2))
        bit *= 2
    return other


def dot_nt(a, b):
    return lax.dot_general(a, b, (((1,), (1,)), ((), ())), preferred_element_type=F32)


def dot_nn(a, b):
    return lax.dot_general(a, b, (((1,), (0,)), ((), ())), preferred_element_type=F32)


def fused(
    n,
    n_mp,
    move_w,
    q_hbm,
    dq_hbm,
    k_hbm,
    v_hbm,
    dk_hbm,
    dv_hbm,
    flags_hbm,
    w_hbm,
    gate_hbm,
    x_hbm,
    dx_hbm,
    out,
    d_out,
    own,
    qcat,
    tkv,
    kv,
    opp,
    m_s,
    l_s,
    c_s,
    a_s,
    g_s,
    ao,
    wbuf,
    acc,
    xbuf,
    flags,
    gate,
    own_sem,
    x_sem,
    small_sem,
    w_local,
    ks,
    kr,
    ws,
    wr,
    as_,
    ar,
):
    rows, width = q_hbm.shape
    heads = width // HD
    cols = out.shape[1]
    half = n // 2
    t = lax.axis_index("tm")
    m = lax.axis_index("mp")
    place = ring_place(t, n)
    right = ring_member((place + 1) % n, n)
    left = ring_member((place + n - 1) % n, n)
    peers = [flipped(m, j) for j in range(n_mp)]
    factor = 1.0 / math.sqrt(HD)

    def lanes(h):
        return slice(h * HD, (h + 1) * HD)

    loads = [
        pltpu.make_async_copy(src, own.at[i], own_sem.at[i])
        for i, src in enumerate((k_hbm, v_hbm, dk_hbm, dv_hbm, q_hbm, dq_hbm))
    ]
    loads.append(pltpu.make_async_copy(flags_hbm, flags, small_sem.at[0]))
    for load in loads:
        load.start()

    barrier = pltpu.get_barrier_semaphore()
    for dev in [(right, m), (left, m)] + [(t, peers[j]) for j in range(1, n_mp)]:
        pl.semaphore_signal(barrier, inc=1, device_id=dev, device_id_type=MESH)
    pl.semaphore_wait(barrier, 1 + n_mp)

    def exists(d, s, p):
        return s < half or (s == half and (p < 2) == (d == 0))

    def kv_copy(h, d, s, p):
        side = slice(d * rows, (d + 1) * rows)
        if s > 1:
            src = kv.at[h, s - 2, p, side]
        elif p < 2:
            src = (k_hbm, v_hbm)[p].at[:, lanes(h)]
        else:
            src = tkv.at[h, p - 2]
        dst = kv.at[h, s - 1, p, side] if s < half else opp.at[h, p]
        return pltpu.make_async_remote_copy(
            src_ref=src,
            dst_ref=dst,
            send_sem=ks.at[h, d, s - 1, p],
            recv_sem=kr.at[h, d, s - 1, p],
            device_id=((right, left)[d], m),
            device_id_type=MESH,
        )

    def send_own(h, pieces):
        for p in pieces:
            for d in (0, 1):
                kv_copy(h, d, 1, p).start()

    def w_copy(h, j):
        span = pl.ds(pl.multiple_of(peers[j] * cols, HD), cols)
        part = slice(h * HD, (h + 1) * HD)
        if j == 0:
            return pltpu.make_async_copy(
                w_hbm.at[part, span], wbuf.at[0, part], w_local.at[h]
            )
        return pltpu.make_async_remote_copy(
            src_ref=w_hbm.at[part, span],
            dst_ref=wbuf.at[j, part],
            send_sem=ws.at[h, j],
            recv_sem=wr.at[h, j],
            device_id=(t, peers[j]),
            device_id_type=MESH,
        )

    def ao_copy(h, j):
        relay = j % 2 == 1 and j > 1
        return pltpu.make_async_remote_copy(
            src_ref=ao.at[h, j - 1 if relay else 0],
            dst_ref=ao.at[h, j],
            send_sem=as_.at[h, j],
            recv_sem=ar.at[h, j],
            device_id=(t, peers[1] if relay else peers[j]),
            device_id_type=MESH,
        )

    send_own(0, (0, 1))
    if move_w:
        for h in range(heads):
            for j in list(range(2, n_mp)) + [1, 0]:
                w_copy(h, j).start()
    x_loads = [
        pltpu.make_async_copy(src, xbuf.at[i], x_sem.at[i])
        for i, src in enumerate((x_hbm, dx_hbm))
    ]
    x_loads.append(pltpu.make_async_copy(gate_hbm, gate, small_sem.at[1]))
    for load in x_loads:
        load.start()
    for load in loads:
        load.wait()

    live = [
        jnp.where(flags[i * FRAME] > 0, 1.0, 0.0).astype(F32)
        for i in range(rows // FRAME)
    ]

    def masked(value, i):
        scale = jnp.full(value.shape, live[i], F32)
        return (value.astype(F32) * scale).astype(BF16)

    for h in range(heads):
        for i in range(rows // FRAME):
            part = slice(i * FRAME, (i + 1) * FRAME)
            tkv[h, 0, part] = masked(own[2, part, lanes(h)], i)
            tkv[h, 1, part] = masked(own[3, part, lanes(h)], i)
        if h == 0:
            send_own(0, (2, 3))
            for g in range(1, heads):
                send_own(g, (0, 1))
        else:
            send_own(h, (2, 3))
    for h in range(heads):
        for i in range(rows // FRAME):
            part = slice(i * FRAME, (i + 1) * FRAME)
            qcat[h, part, 0:HD] = masked(own[5, part, lanes(h)], i)
        qcat[h, :, HD : 2 * HD] = own[4, :, lanes(h)]

    def attend(h, k, tk, values, first):
        queries = qcat[h, :, HD : 2 * HD]
        scores = dot_nt(queries, k)
        d_scores = dot_nt(qcat[h], jnp.concatenate([k, tk], axis=1)) * factor
        peak = jnp.max(scores, axis=1, keepdims=True)
        if not first:
            peak_old = m_s[h]
            peak = jnp.maximum(peak_old, peak)
            rescale = jnp.exp((peak_old - peak) * factor)
        weights = jnp.exp((scores - peak) * factor)
        product = weights * d_scores
        total = jnp.sum(weights, axis=1, keepdims=True)
        slope = jnp.sum(product, axis=1, keepdims=True)
        weights_b = weights.astype(BF16)
        product_b = product.astype(BF16)
        v, tv = values()
        primal = dot_nn(weights_b, v)
        tangent = dot_nn(product_b, v) + dot_nn(weights_b, tv)
        m_s[h] = peak
        if first:
            l_s[h] = total
            c_s[h] = slope
            a_s[h] = primal
            g_s[h] = tangent
        else:
            l_s[h] = l_s[h] * rescale + total
            c_s[h] = c_s[h] * rescale + slope
            a_s[h] = a_s[h] * rescale + primal
            g_s[h] = g_s[h] * rescale + tangent

    def finish(h):
        inverse = 1.0 / l_s[h]
        outputs = a_s[h] * inverse
        d_outputs = g_s[h] * inverse - (c_s[h] * inverse) * outputs
        ao[h, 0, 0:rows] = outputs.astype(BF16)
        ao[h, 0, rows : 2 * rows] = d_outputs.astype(BF16)
        for j in list(range(2, n_mp, 2)) + [1]:
            ao_copy(h, j).start()

    def relay(h):
        for j in range(2, n_mp, 2):
            ao_copy(h, j).wait_recv()
            ao_copy(h, j + 1).start()

    for h in range(heads):
        attend(
            h, own[0, :, lanes(h)], tkv[h, 0], lambda: (own[1, :, lanes(h)], tkv[h, 1]), True
        )
    for s in range(1, half):
        for h in range(heads):
            for p in range(4):
                for d in (0, 1):
                    kv_copy(h, d, s, p).wait_recv()
                    if exists(d, s + 1, p):
                        kv_copy(h, d, s + 1, p).start()
            attend(
                h,
                kv[h, s - 1, 0],
                kv[h, s - 1, 2],
                lambda: (kv[h, s - 1, 1], kv[h, s - 1, 3]),
                False,
            )
    for h in range(heads):
        def opposite(first_p, second_p):
            kv_copy(h, 0, half, first_p).wait_recv()
            kv_copy(h, 1, half, second_p).wait_recv()
            return opp[h, first_p], opp[h, second_p]

        keys, d_keys = opposite(0, 2)
        attend(h, keys, d_keys, lambda: opposite(1, 3), False)
        finish(h)

    step = 2 * HD if cols % (2 * HD) == 0 else cols
    chunks = [slice(c, c + step) for c in range(0, cols, step)]

    def w_part(h, j, chunk):
        part = slice(h * HD, (h + 1) * HD)
        if move_w:
            return wbuf[j, part, chunk]
        return w_hbm[peers[j], part, chunk]

    def project(slots, chunk):
        attn = jnp.concatenate([ao[h, j] for h, j in slots], axis=1)
        weight = jnp.concatenate([w_part(h, j, chunk) for h, j in slots], axis=0)
        return dot_nn(attn, weight)

    if move_w:
        for h in range(heads):
            w_copy(h, 0).wait()
            for j in range(1, n_mp):
                w_copy(h, j).wait_recv()
    for load in x_loads:
        load.wait()
    last = heads - 1
    for h in range(heads):
        ao_copy(h, 1).wait_recv()
    near = [(h, j) for h in range(heads) for j in (0, 1)]
    for chunk in chunks:
        acc[:, chunk] = project(near, chunk)
    for h in range(last):
        relay(h)
    for h in range(last):
        for j in range(3, n_mp, 2):
            ao_copy(h, j).wait_recv()
    far = [(h, j) for h in range(last) for j in range(2, n_mp)]
    for chunk in chunks:
        acc[:, chunk] += project(far, chunk)
    for h in range(heads):
        for s in range(1, half + 1):
            for p in range(4):
                for d in (0, 1):
                    if exists(d, s, p):
                        kv_copy(h, d, s, p).wait_send()
        if move_w:
            for j in range(1, n_mp):
                w_copy(h, j).wait_send()
    relay(last)
    even = [(last, j) for j in range(2, n_mp, 2)]
    for chunk in chunks:
        acc[:, chunk] += project(even, chunk)
    for j in range(3, n_mp, 2):
        ao_copy(last, j).wait_recv()
    odd = [(last, j) for j in range(3, n_mp, 2)]
    for chunk in chunks:
        part = acc[:, chunk] + project(odd, chunk)
        scale = gate[chunk].reshape(1, step)
        out[:, chunk] = (xbuf[0, :, chunk].astype(F32) + scale * part[0:rows]).astype(BF16)
        for i in range(rows // FRAME):
            piece = slice(i * FRAME, (i + 1) * FRAME)
            base = xbuf[1, piece, chunk].astype(F32)
            base = base * jnp.full(base.shape, live[i], F32)
            delta = part[rows + i * FRAME : rows + (i + 1) * FRAME]
            d_out[piece, chunk] = (base + scale * delta).astype(BF16)

    for h in range(heads):
        for j in range(1, n_mp):
            ao_copy(h, j).wait_send()


def per_device(n, n_mp, q, dq, k, v, dk, dv, flags, w, gate, x, dx):
    rows, width = q.shape
    cols = x.shape[1]
    heads = width // HD
    half = n // 2
    move_w = cols % HD == 0
    if not move_w:
        w = lax.all_to_all(w, "mp", split_axis=1, concat_axis=0, tiled=True)
        w = w.reshape(n_mp, width, cols)
    anywhere = pl.BlockSpec(memory_space=pl.ANY)
    vmem = pl.BlockSpec(memory_space=pltpu.VMEM)
    dma = pltpu.SemaphoreType.DMA
    return pl.pallas_call(
        functools.partial(fused, n, n_mp, move_w),
        out_shape=(pltpu.VMEM(x.shape, BF16), pltpu.VMEM(x.shape, BF16)),
        in_specs=[anywhere] * 6
        + [anywhere, anywhere if move_w else vmem, anywhere]
        + [anywhere] * 2,
        out_specs=(vmem, vmem),
        scratch_shapes=[
            pltpu.VMEM((6, rows, width), BF16),
            pltpu.VMEM((heads, rows, 2 * HD), BF16),
            pltpu.VMEM((heads, 2, rows, HD), BF16),
            pltpu.VMEM((heads, half - 1, 4, 2 * rows, HD), BF16),
            pltpu.VMEM((heads, 4, rows, HD), BF16),
            pltpu.VMEM((heads, rows, 1), F32),
            pltpu.VMEM((heads, rows, 1), F32),
            pltpu.VMEM((heads, rows, 1), F32),
            pltpu.VMEM((heads, rows, HD), F32),
            pltpu.VMEM((heads, rows, HD), F32),
            pltpu.VMEM((heads, n_mp, 2 * rows, HD), BF16),
            pltpu.VMEM((n_mp, width, cols) if move_w else (1, 16, HD), BF16),
            pltpu.VMEM((2 * rows, cols), F32),
            pltpu.VMEM((2, rows, cols), BF16),
            pltpu.SMEM((rows,), jnp.int32),
            pltpu.VMEM((cols,), F32),
            dma((6,)),
            dma((2,)),
            dma((2,)),
            dma((heads,)),
            dma((heads, 2, half, 4)),
            dma((heads, 2, half, 4)),
            dma((heads, n_mp)),
            dma((heads, n_mp)),
            dma((heads, n_mp)),
            dma((heads, n_mp)),
        ],
        compiler_params=pltpu.CompilerParams(
            collective_id=0, has_side_effects=True, vmem_limit_bytes=65000000
        ),
    )(q, dq, k, v, dk, dv, flags, w, gate, x, dx)


def solution(mesh):
    both = P("tm", "mp")
    placed = (both,) * 6 + (P("tm"), P("mp", None), P("mp"), both, both)
    return jax.shard_map(
        functools.partial(per_device, mesh.shape["tm"], mesh.shape["mp"]),
        mesh=mesh,
        in_specs=placed,
        out_specs=(both, both),
        check_vma=False,
    )
```

```python
import functools
import math

import jax
import jax.numpy as jnp
from jax import lax
from jax.experimental import pallas as pl
from jax.experimental.pallas import tpu as pltpu
from jax.sharding import PartitionSpec as P

HD = 128
FRAME = 32
MESH = pl.DeviceIdType.MESH
F32 = jnp.float32
BF16 = jnp.bfloat16


def ring_place(t, n):
    return jnp.where(t % 2 == 0, t // 2, n - 1 - t // 2)


def ring_member(r, n):
    return jnp.where(r < n // 2, 2 * r, 2 * (n - 1 - r) + 1)


def flipped(me, j):
    other = me
    bit = 1
    while bit <= j:
        if j & bit:
            other = other + bit * (1 - 2 * ((me // bit) % 2))
        bit *= 2
    return other


def dot_nt(a, b):
    return lax.dot_general(a, b, (((1,), (1,)), ((), ())), preferred_element_type=F32)


def dot_nn(a, b):
    return lax.dot_general(a, b, (((1,), (0,)), ((), ())), preferred_element_type=F32)


def fused(
    n,
    n_mp,
    move_w,
    q_hbm,
    dq_hbm,
    k_hbm,
    v_hbm,
    dk_hbm,
    dv_hbm,
    flags_hbm,
    w_hbm,
    gate_hbm,
    x_hbm,
    dx_hbm,
    out,
    d_out,
    own,
    qcat,
    tkv,
    kv,
    opp,
    m_s,
    l_s,
    c_s,
    a_s,
    g_s,
    ao,
    wbuf,
    acc,
    xbuf,
    flags,
    gate,
    own_sem,
    x_sem,
    small_sem,
    w_local,
    ks,
    kr,
    ws,
    wr,
    as_,
    ar,
):
    rows, width = q_hbm.shape
    heads = width // HD
    cols = out.shape[1]
    half = n // 2
    t = lax.axis_index("tm")
    m = lax.axis_index("mp")
    place = ring_place(t, n)
    right = ring_member((place + 1) % n, n)
    left = ring_member((place + n - 1) % n, n)
    peers = [flipped(m, j) for j in range(n_mp)]
    factor = 1.0 / math.sqrt(HD)

    def lanes(h):
        return slice(h * HD, (h + 1) * HD)

    loads = [
        pltpu.make_async_copy(src, own.at[i], own_sem.at[i])
        for i, src in enumerate((k_hbm, v_hbm, dk_hbm, dv_hbm, q_hbm, dq_hbm))
    ]
    loads.append(pltpu.make_async_copy(flags_hbm, flags, small_sem.at[0]))
    for load in loads:
        load.start()

    barrier = pltpu.get_barrier_semaphore()
    for dev in [(right, m), (left, m)] + [(t, peers[j]) for j in range(1, n_mp)]:
        pl.semaphore_signal(barrier, inc=1, device_id=dev, device_id_type=MESH)
    pl.semaphore_wait(barrier, 1 + n_mp)

    def exists(d, s, p):
        return s < half or (s == half and (p < 2) == (d == 0))

    def kv_copy(h, d, s, p):
        side = slice(d * rows, (d + 1) * rows)
        if s > 1:
            src = kv.at[h, s - 2, p, side]
        elif p < 2:
            src = (k_hbm, v_hbm)[p].at[:, lanes(h)]
        else:
            src = tkv.at[h, p - 2]
        dst = kv.at[h, s - 1, p, side] if s < half else opp.at[h, p]
        return pltpu.make_async_remote_copy(
            src_ref=src,
            dst_ref=dst,
            send_sem=ks.at[h, d, s - 1, p],
            recv_sem=kr.at[h, d, s - 1, p],
            device_id=((right, left)[d], m),
            device_id_type=MESH,
        )

    def send_own(h, pieces):
        for p in pieces:
            for d in (0, 1):
                kv_copy(h, d, 1, p).start()

    def w_copy(h, j):
        span = pl.ds(pl.multiple_of(peers[j] * cols, HD), cols)
        part = slice(h * HD, (h + 1) * HD)
        if j == 0:
            return pltpu.make_async_copy(
                w_hbm.at[part, span], wbuf.at[0, part], w_local.at[h]
            )
        return pltpu.make_async_remote_copy(
            src_ref=w_hbm.at[part, span],
            dst_ref=wbuf.at[j, part],
            send_sem=ws.at[h, j],
            recv_sem=wr.at[h, j],
            device_id=(t, peers[j]),
            device_id_type=MESH,
        )

    def ao_copy(h, j):
        relay = j % 2 == 1 and j > 1
        return pltpu.make_async_remote_copy(
            src_ref=ao.at[h, j - 1 if relay else 0],
            dst_ref=ao.at[h, j],
            send_sem=as_.at[h, j],
            recv_sem=ar.at[h, j],
            device_id=(t, peers[1] if relay else peers[j]),
            device_id_type=MESH,
        )

    send_own(0, (0, 1))
    if move_w:
        for h in range(heads):
            for j in list(range(2, n_mp)) + [1, 0]:
                w_copy(h, j).start()
    x_loads = [
        pltpu.make_async_copy(src, xbuf.at[i], x_sem.at[i])
        for i, src in enumerate((x_hbm, dx_hbm))
    ]
    x_loads.append(pltpu.make_async_copy(gate_hbm, gate, small_sem.at[1]))
    for load in x_loads:
        load.start()
    for load in loads:
        load.wait()

    live = [
        jnp.where(flags[i * FRAME] > 0, 1.0, 0.0).astype(F32)
        for i in range(rows // FRAME)
    ]

    def masked(value, i):
        scale = jnp.full(value.shape, live[i], F32)
        return (value.astype(F32) * scale).astype(BF16)

    for h in range(heads):
        for i in range(rows // FRAME):
            part = slice(i * FRAME, (i + 1) * FRAME)
            tkv[h, 0, part] = masked(own[2, part, lanes(h)], i)
            tkv[h, 1, part] = masked(own[3, part, lanes(h)], i)
        if h == 0:
            send_own(0, (2, 3))
            for g in range(1, heads):
                send_own(g, (0, 1))
        else:
            send_own(h, (2, 3))
    for h in range(heads):
        for i in range(rows // FRAME):
            part = slice(i * FRAME, (i + 1) * FRAME)
            qcat[h, part, 0:HD] = masked(own[5, part, lanes(h)], i)
        qcat[h, :, HD : 2 * HD] = own[4, :, lanes(h)]

    def attend(h, k, tk, values, first):
        queries = qcat[h, :, HD : 2 * HD]
        scores = dot_nt(queries, k)
        d_scores = dot_nt(qcat[h], jnp.concatenate([k, tk], axis=1)) * factor
        peak = jnp.max(scores, axis=1, keepdims=True)
        if not first:
            peak_old = m_s[h]
            peak = jnp.maximum(peak_old, peak)
            rescale = jnp.exp((peak_old - peak) * factor)
        weights = jnp.exp((scores - peak) * factor)
        product = weights * d_scores
        total = jnp.sum(weights, axis=1, keepdims=True)
        slope = jnp.sum(product, axis=1, keepdims=True)
        weights_b = weights.astype(BF16)
        product_b = product.astype(BF16)
        v, tv = values()
        primal = dot_nn(weights_b, v)
        tangent = dot_nn(product_b, v) + dot_nn(weights_b, tv)
        m_s[h] = peak
        if first:
            l_s[h] = total
            c_s[h] = slope
            a_s[h] = primal
            g_s[h] = tangent
        else:
            l_s[h] = l_s[h] * rescale + total
            c_s[h] = c_s[h] * rescale + slope
            a_s[h] = a_s[h] * rescale + primal
            g_s[h] = g_s[h] * rescale + tangent

    def finish(h):
        inverse = 1.0 / l_s[h]
        outputs = a_s[h] * inverse
        d_outputs = g_s[h] * inverse - (c_s[h] * inverse) * outputs
        ao[h, 0, 0:rows] = outputs.astype(BF16)
        ao[h, 0, rows : 2 * rows] = d_outputs.astype(BF16)
        for j in list(range(2, n_mp, 2)) + [1]:
            ao_copy(h, j).start()

    def relay(h):
        for j in range(2, n_mp, 2):
            ao_copy(h, j).wait_recv()
            ao_copy(h, j + 1).start()

    for h in range(heads):
        attend(
            h, own[0, :, lanes(h)], tkv[h, 0], lambda: (own[1, :, lanes(h)], tkv[h, 1]), True
        )
    for s in range(1, half):
        for h in range(heads):
            for p in range(4):
                for d in (0, 1):
                    kv_copy(h, d, s, p).wait_recv()
                    if exists(d, s + 1, p):
                        kv_copy(h, d, s + 1, p).start()
        for h in range(heads):
            attend(
                h,
                kv[h, s - 1, 0],
                kv[h, s - 1, 2],
                lambda: (kv[h, s - 1, 1], kv[h, s - 1, 3]),
                False,
            )
    for h in range(heads):
        def opposite(first_p, second_p):
            kv_copy(h, 0, half, first_p).wait_recv()
            kv_copy(h, 1, half, second_p).wait_recv()
            return opp[h, first_p], opp[h, second_p]

        keys, d_keys = opposite(0, 2)
        attend(h, keys, d_keys, lambda: opposite(1, 3), False)
        finish(h)

    step = 2 * HD if cols % (2 * HD) == 0 else cols
    chunks = [slice(c, c + step) for c in range(0, cols, step)]

    def w_part(h, j, chunk):
        part = slice(h * HD, (h + 1) * HD)
        if move_w:
            return wbuf[j, part, chunk]
        return w_hbm[peers[j], part, chunk]

    def project(slots, chunk):
        attn = jnp.concatenate([ao[h, j] for h, j in slots], axis=1)
        weight = jnp.concatenate([w_part(h, j, chunk) for h, j in slots], axis=0)
        return dot_nn(attn, weight)

    if move_w:
        for h in range(heads):
            w_copy(h, 0).wait()
            for j in range(1, n_mp):
                w_copy(h, j).wait_recv()
    for load in x_loads:
        load.wait()
    last = heads - 1
    for h in range(heads):
        ao_copy(h, 1).wait_recv()
    near = [(h, j) for h in range(heads) for j in (0, 1)]
    for chunk in chunks:
        acc[:, chunk] = project(near, chunk)
    for h in range(last):
        relay(h)
    for h in range(last):
        for j in range(3, n_mp, 2):
            ao_copy(h, j).wait_recv()
    far = [(h, j) for h in range(last) for j in range(2, n_mp)]
    for chunk in chunks:
        acc[:, chunk] += project(far, chunk)
    for h in range(heads):
        for s in range(1, half + 1):
            for p in range(4):
                for d in (0, 1):
                    if exists(d, s, p):
                        kv_copy(h, d, s, p).wait_send()
        if move_w:
            for j in range(1, n_mp):
                w_copy(h, j).wait_send()
    relay(last)
    even = [(last, j) for j in range(2, n_mp, 2)]
    for chunk in chunks:
        acc[:, chunk] += project(even, chunk)
    for j in range(3, n_mp, 2):
        ao_copy(last, j).wait_recv()
    odd = [(last, j) for j in range(3, n_mp, 2)]
    for chunk in chunks:
        part = acc[:, chunk] + project(odd, chunk)
        scale = gate[chunk].reshape(1, step)
        out[:, chunk] = (xbuf[0, :, chunk].astype(F32) + scale * part[0:rows]).astype(BF16)
        for i in range(rows // FRAME):
            piece = slice(i * FRAME, (i + 1) * FRAME)
            base = xbuf[1, piece, chunk].astype(F32)
            base = base * jnp.full(base.shape, live[i], F32)
            delta = part[rows + i * FRAME : rows + (i + 1) * FRAME]
            d_out[piece, chunk] = (base + scale * delta).astype(BF16)

    for h in range(heads):
        for j in range(1, n_mp):
            ao_copy(h, j).wait_send()


def per_device(n, n_mp, q, dq, k, v, dk, dv, flags, w, gate, x, dx):
    rows, width = q.shape
    cols = x.shape[1]
    heads = width // HD
    half = n // 2
    move_w = cols % HD == 0
    if not move_w:
        w = lax.all_to_all(w, "mp", split_axis=1, concat_axis=0, tiled=True)
        w = w.reshape(n_mp, width, cols)
    anywhere = pl.BlockSpec(memory_space=pl.ANY)
    vmem = pl.BlockSpec(memory_space=pltpu.VMEM)
    dma = pltpu.SemaphoreType.DMA
    return pl.pallas_call(
        functools.partial(fused, n, n_mp, move_w),
        out_shape=(pltpu.VMEM(x.shape, BF16), pltpu.VMEM(x.shape, BF16)),
        in_specs=[anywhere] * 6
        + [anywhere, anywhere if move_w else vmem, anywhere]
        + [anywhere] * 2,
        out_specs=(vmem, vmem),
        scratch_shapes=[
            pltpu.VMEM((6, rows, width), BF16),
            pltpu.VMEM((heads, rows, 2 * HD), BF16),
            pltpu.VMEM((heads, 2, rows, HD), BF16),
            pltpu.VMEM((heads, half - 1, 4, 2 * rows, HD), BF16),
            pltpu.VMEM((heads, 4, rows, HD), BF16),
            pltpu.VMEM((heads, rows, 1), F32),
            pltpu.VMEM((heads, rows, 1), F32),
            pltpu.VMEM((heads, rows, 1), F32),
            pltpu.VMEM((heads, rows, HD), F32),
            pltpu.VMEM((heads, rows, HD), F32),
            pltpu.VMEM((heads, n_mp, 2 * rows, HD), BF16),
            pltpu.VMEM((n_mp, width, cols) if move_w else (1, 16, HD), BF16),
            pltpu.VMEM((2 * rows, cols), F32),
            pltpu.VMEM((2, rows, cols), BF16),
            pltpu.SMEM((rows,), jnp.int32),
            pltpu.VMEM((cols,), F32),
            dma((6,)),
            dma((2,)),
            dma((2,)),
            dma((heads,)),
            dma((heads, 2, half, 4)),
            dma((heads, 2, half, 4)),
            dma((heads, n_mp)),
            dma((heads, n_mp)),
            dma((heads, n_mp)),
            dma((heads, n_mp)),
        ],
        compiler_params=pltpu.CompilerParams(
            collective_id=0, has_side_effects=True, vmem_limit_bytes=65000000
        ),
    )(q, dq, k, v, dk, dv, flags, w, gate, x, dx)


def solution(mesh):
    both = P("tm", "mp")
    placed = (both,) * 6 + (P("tm"), P("mp", None), P("mp"), both, both)
    return jax.shard_map(
        functools.partial(per_device, mesh.shape["tm"], mesh.shape["mp"]),
        mesh=mesh,
        in_specs=placed,
        out_specs=(both, both),
        check_vma=False,
    )
```
